32 devices in a mesh: panel: 2 (over y), dom: 4 (over z), blk: 2 (over x), dir: 2 (over core).
Axes of the slice: x: 2, y: 2, z: 4, core: 2. Of those that a mesh axis runs over, the one named last changes fastest.
Arguments:
- panel_vectors: bfloat16 [3072, 2048], P('dom', ('panel', 'blk')), parts along dimension 1, may hold values from -6 to 6
- force_blocks: float32 [16, 9, 1024], P(None, None, 'dom'), may hold values from -1 to 1
- bond_vectors: float32 [2, 16, 1024], P('dir', None, 'dom'), may hold values from -4 to 4
- neighbours: int32 [16, 1024], P(None, 'dom'), may hold values from 0 to 511
- boundary_low: int32 [512], P('dom'), may hold values from 0 to 255
- boundary_high: int32 [512], P('dom'), may hold values from 0 to 255
Outputs:
- coupling: float32 [2, 2048, 1024], P('dir', ('panel', 'dom'), 'blk'), parts along dimension 1
The draws below stay inside these ranges and needn't reach their ends.
There are 2 independent parts, one for each index of `panel`. The reference program is written for one: setup_inputs(seed, part) draws one part's arguments, and reference() takes and returns one part's arrays. A program takes and returns all parts, laid end to end along the dimension named above; an argument that names none is the same for every part. Nothing has to cross between parts.
Inputs may be any that keep to these rules, and one draw needn't show every extreme that they name: `neighbours`: an entry below 256 names an atom of the same domain; from 256 to 383 the listed boundary atoms of the domain below; from 384 on those of the domain above. `boundary_low`: local atom numbers within the domain that owns the block; repeats may occur. `boundary_high`: local atom numbers within the domain that owns the block; repeats may occur.
All inputs are finite; a program needn't handle non-finite values.
Results may differ from the reference program's by a relative error of at most 0.0029.
Values may be sent and summed in bfloat16 or wider, within the bound.
A program may use at most 64 MiB of HBM per device.

```python
import jax
import jax.numpy as jnp
from jax import lax

AD = 256
M = 1024
K = 16
BND = 128
ATOMS = 1024
N_DOM = 4


def set_ends(entries, stream_key, least, top_value):
    longest = entries.shape.index(max(entries.shape))
    spots = []
    for shift in (0, 1):
        where = [jax.random.randint(jax.random.fold_in(stream_key, axis), (), 0, length) for axis, length in enumerate(entries.shape)]
        where[longest] = (where[longest] + shift) % entries.shape[longest]
        spots.append(tuple(where))
    return entries.at[spots[0]].set(least).at[spots[1]].set(top_value)


def block_levels(rng, shape, shards, smallest, high):
    level = 1.0
    for position, blocks in shards:
        draws = jax.random.uniform(jax.random.fold_in(jax.random.fold_in(rng, 6), position), (blocks,), jnp.float32, smallest / len(shards), high / len(shards))
        level = level * jnp.repeat(jnp.exp(draws), shape[position] // blocks).reshape((-1,) + (1,) * (len(shape) - 1 - position))
    return level


def noise(key, extent, spread, reach, shards=(), kind=jnp.bfloat16):
    drawn = spread * jax.random.normal(key, extent, jnp.float32)
    if shards:
        drawn = drawn * block_levels(key, extent, shards, -0.22, 0.18)
    return jnp.clip(drawn, -reach, reach).astype(kind)


def setup_inputs(seed: int = 0, part: int = 0) -> dict:
    streams_of = jax.random.split(jax.random.key(seed), 7)
    own_keys = jax.random.split(jax.random.fold_in(streams_of[6], part), 7)
    return {
        "panel_vectors": noise(own_keys[0], (3 * ATOMS, M), 1.0, 6.0, ((0, 4), (1, 2))),
        "force_blocks": noise(streams_of[1], (K, 9, ATOMS), 0.15, 1.0, ((2, 4),), jnp.float32),
        "bond_vectors": noise(streams_of[2], (2, K, ATOMS), 1.0, 4.0, ((0, 2), (2, 4)), jnp.float32),
        "neighbours": set_ends(jax.random.randint(streams_of[3], (K, ATOMS), 0, AD + 2 * BND), jax.random.fold_in(streams_of[3], 1), 0, (AD + 2 * BND) - 1).astype(jnp.int32),
        "boundary_low": set_ends(jax.random.randint(streams_of[4], (BND * N_DOM,), 0, AD), jax.random.fold_in(streams_of[4], 1), 0, AD - 1).astype(jnp.int32),
        "boundary_high": set_ends(jax.random.randint(streams_of[5], (BND * N_DOM,), 0, AD), jax.random.fold_in(streams_of[5], 1), 0, AD - 1).astype(jnp.int32),
    }


def flux_of(ext, forces, bond, nbrs):
    weights = forces * bond[:, None, :]
    atoms = nbrs.shape[1]

    def step(total, k):
        gathered = ext[nbrs[k]].astype(jnp.float32)
        blocks = weights[k].reshape(3, 3, atoms).transpose(2, 0, 1)
        return total + jnp.sum(blocks[:, :, :, None] * gathered[:, None, :, :], axis=2), None

    init = jnp.zeros((atoms, 3, ext.shape[2]), jnp.float32)
    total, unused = lax.scan(step, init, jnp.arange(K, dtype=jnp.int32))
    return total


def reference(panel_vectors, force_blocks, bond_vectors, neighbours, boundary_low, boundary_high):
    stacked = panel_vectors.reshape(N_DOM, AD, 3, M)

    def domain(d, coupling):
        prev = jnp.mod(d - 1 + N_DOM, N_DOM).astype(jnp.int32)
        nextd = jnp.mod(d + 1, N_DOM).astype(jnp.int32)
        own = lax.dynamic_slice_in_dim(stacked, d, 1, 0)[0]
        low_src = lax.dynamic_slice_in_dim(stacked, prev, 1, 0)[0]
        high_src = lax.dynamic_slice_in_dim(stacked, nextd, 1, 0)[0]
        upper_list = lax.dynamic_slice_in_dim(boundary_high, (prev * BND).astype(jnp.int32), BND, 0)
        lower_list = lax.dynamic_slice_in_dim(boundary_low, (nextd * BND).astype(jnp.int32), BND, 0)
        ext = jnp.concatenate([own, low_src[upper_list], high_src[lower_list]], axis=0)
        start = (d * AD).astype(jnp.int32)
        forces = lax.dynamic_slice_in_dim(force_blocks, start, AD, 2)
        bonds = lax.dynamic_slice_in_dim(bond_vectors, start, AD, 2)
        nbrs = lax.dynamic_slice_in_dim(neighbours, start, AD, 1)
        own_rows = own.reshape(3 * AD, M)
        parts = []
        for c in range(2):
            flux = flux_of(ext, forces, bonds[c], nbrs).astype(jnp.bfloat16).reshape(3 * AD, M)
            parts.append(jnp.dot(own_rows.T, flux, preferred_element_type=jnp.float32))
        return coupling + jnp.stack(parts, axis=0)

    coupling = lax.fori_loop(0, N_DOM, domain, jnp.zeros((2, M, M), jnp.float32))
    return coupling * ((3.0 * ATOMS) ** -0.5)
```

```python
import functools

import jax
import jax.numpy as jnp
from jax import lax
from jax.experimental import pallas as pl
from jax.experimental.pallas import tpu as pltpu
from jax.sharding import PartitionSpec as P

MESH = pl.DeviceIdType.MESH
BF16 = jnp.bfloat16
F32 = jnp.float32


def one_hot(hits):
    return jnp.where(hits, 1.0, 0.0).astype(BF16)


def dot(a, b):
    return jnp.dot(a, b, preferred_element_type=F32)


def kernel(n, nblk, v_ref, force_ref, bond_ref, nbr_ref, low_ref, high_ref, out_ref,
           vt, vx, hs, ht, w, st_hi, st_lo, flux, ft, part, su, ru, sd, rd,
           h_send, h_recv, hf_send, hf_recv, x_send, x_recv, xf_send, xf_recv,
           u_send, u_recv, d_send, d_recv):
    me = lax.axis_index("dom")
    blk = lax.axis_index("blk")
    core = lax.axis_index("dir")
    rows, cols = v_ref.shape
    atoms = rows // 3
    half = cols // 2
    bnd = low_ref.shape[1]
    steps = nbr_ref.shape[0]
    tile = out_ref.shape[0]
    up, down = lax.rem(me + 1, n), lax.rem(me + n - 1, n)
    peers = [{"dom": up}, {"dom": down}, {"dir": 1 - core}]
    peers += [{"blk": lax.rem(blk + o, nblk)} for o in range(1, nblk)]

    barrier = pltpu.get_barrier_semaphore()
    for peer in peers:
        pl.semaphore_signal(barrier, inc=1, device_id=peer, device_id_type=MESH)

    vt[...] = v_ref[...].T
    mine = vt[pl.ds(pl.multiple_of(core * half, half), half), :]
    atom_row = lax.broadcasted_iota(jnp.int32, (rows, bnd), 0)
    for side, list_ref in ((0, high_ref), (1, low_ref)):
        for b in range(3):
            pick = one_hot(atom_row == 3 * list_ref[...] + b)
            hs[side, b] = dot(mine, pick).astype(BF16)
    pl.semaphore_wait(barrier, len(peers))

    halo = [
        pltpu.make_async_remote_copy(
            src_ref=hs.at[side], dst_ref=ht.at[side, core],
            send_sem=h_send.at[side], recv_sem=h_recv.at[side],
            device_id={"dom": up if side == 0 else down}, device_id_type=MESH)
        for side in range(2)
    ]
    for copy in halo:
        copy.start()

    row_of = lax.broadcasted_iota(jnp.int32, (rows, atoms), 0)
    atom_of = lax.broadcasted_iota(jnp.int32, (rows, atoms), 1)
    for a in range(3):
        pick = one_hot(row_of == 3 * atom_of + a)
        for h in range(2):
            vx[blk, h, :, a * atoms:(a + 1) * atoms] = dot(vt[h * half:(h + 1) * half, :], pick).astype(BF16)

    tiles = [
        pltpu.make_async_remote_copy(
            src_ref=vx.at[blk, core], dst_ref=vx.at[blk, core],
            send_sem=x_send.at[o - 1], recv_sem=x_recv.at[o - 1],
            device_id={"blk": lax.rem(blk + o, nblk)}, device_id_type=MESH)
        for o in range(1, nblk)
    ]
    for copy in tiles:
        copy.start()

    for k in range(steps):
        w[k] = force_ref[k] * bond_ref[0, k:k + 1, :]
    group = 16
    lanes = min(atoms, 256)

    def build(t, carry):
        j0 = pl.multiple_of(t * group, group)
        region = t // (atoms // group)
        base = pl.multiple_of(region * rows + (j0 - region * atoms), group)
        for i0 in range(0, atoms, lanes):
            js = lax.broadcasted_iota(jnp.int32, (group, lanes), 0) + j0
            total = [jnp.zeros((group, lanes), F32) for _ in range(9)]
            for k in range(steps):
                hit = js == nbr_ref[k:k + 1, i0:i0 + lanes]
                for q in range(9):
                    total[q] = total[q] + jnp.where(hit, w[k, q:q + 1, i0:i0 + lanes], 0.0)
            for a in range(3):
                for b in range(3):
                    value = total[3 * a + b]
                    high = value.astype(BF16)
                    at = (pl.ds(pl.multiple_of(base + b * atoms, group), group),
                          slice(a * atoms + i0, a * atoms + i0 + lanes))
                    st_hi[at] = high
                    st_lo[at] = (value - high.astype(F32)).astype(BF16)
        return carry

    lax.fori_loop(0, (atoms + 2 * bnd) // group, build, 0)

    for h in range(2):
        own = vx[blk, h]
        flux[h] = dot(own, st_hi[:rows, :]) + dot(own, st_lo[:rows, :])

    halo_on = []
    for side in range(2):
        halo[side].wait_recv()
        copy = pltpu.make_async_remote_copy(
            src_ref=ht.at[side, core], dst_ref=ht.at[side, core],
            send_sem=hf_send.at[side], recv_sem=hf_recv.at[side],
            device_id={"dir": 1 - core}, device_id_type=MESH)
        copy.start()
        halo_on.append(copy)
    tiles_on = []
    for o in range(1, nblk):
        tiles[o - 1].wait_recv()
        source = lax.rem(blk + nblk - o, nblk)
        copy = pltpu.make_async_remote_copy(
            src_ref=vx.at[source, core], dst_ref=vx.at[source, core],
            send_sem=xf_send.at[o - 1], recv_sem=xf_recv.at[o - 1],
            device_id={"dir": 1 - core}, device_id_type=MESH)
        copy.start()
        tiles_on.append(copy)
    for copy in halo_on:
        copy.wait_recv()
    for h in range(2):
        outer = jnp.concatenate([ht[side, h, b] for b in range(3) for side in range(2)], axis=1)
        total = flux[h] + dot(outer, st_hi[rows:, :]) + dot(outer, st_lo[rows:, :])
        ft[h * half:(h + 1) * half, :] = total.astype(BF16)

    for copy in tiles_on:
        copy.wait_recv()
    for b in range(nblk):
        for h in range(2):
            first = b * cols + h * half
            part[first:first + half, :] = lax.dot_general(
                vx[b, h], ft[...], (((1,), (1,)), ((), ())), preferred_element_type=F32)

    def term(e):
        return part[pl.ds(pl.multiple_of(e * tile, tile), tile), :]

    def hop(e, out, into, send, recv, target):
        return pltpu.make_async_remote_copy(
            src_ref=out.at[e], dst_ref=into.at[e], send_sem=send.at[e], recv_sem=recv.at[e],
            device_id={"dom": target}, device_id_type=MESH)

    def rising(e):
        return hop(e, su, ru, u_send, u_recv, up)

    def falling(e):
        return hop(e, sd, rd, d_send, d_recv, down)

    for t in range(n - 1):
        for first, away, make, out, into in (
            (me, n - 1 - (t - me), rising, su, ru),
            (n - 1 - me, t - (n - 1 - me), falling, sd, rd),
        ):
            @pl.when(first <= t)
            def _(first=first, e=away, make=make, out=out, into=into):
                @pl.when(first == 0)
                def _():
                    out[e] = term(e).astype(out.dtype)

                @pl.when(first > 0)
                def _():
                    make(e).wait_recv()
                    out[e] = (term(e) + into[e].astype(F32)).astype(out.dtype)

                make(e).start()

    out_ref[...] = term(me)

    @pl.when(me > 0)
    def _():
        rising(me).wait_recv()
        out_ref[...] += ru[me].astype(F32)

    @pl.when(me < n - 1)
    def _():
        falling(me).wait_recv()
        out_ref[...] += rd[me].astype(F32)

    for t in range(n - 1):
        @pl.when(me <= t)
        def _(t=t):
            rising(n - 1 - (t - me)).wait_send()

        @pl.when(n - 1 - me <= t)
        def _(t=t):
            falling(t - (n - 1 - me)).wait_send()

    for copy in halo + halo_on + tiles + tiles_on:
        copy.wait_send()


def per_device(n, nblk, panel_vectors, force_blocks, bond_vectors, neighbours, boundary_low, boundary_high):
    rows, cols = panel_vectors.shape
    atoms = rows // 3
    half = cols // 2
    bnd = boundary_low.shape[0]
    steps = neighbours.shape[0]
    tile = nblk * cols // n
    wire = BF16 if n <= 4 else F32
    vmem = pl.BlockSpec(memory_space=pltpu.VMEM)
    line = pltpu.VMEM((n, tile, cols), wire)
    dma = pltpu.SemaphoreType.DMA
    result = pl.pallas_call(
        functools.partial(kernel, n, nblk),
        out_shape=jax.ShapeDtypeStruct((tile, cols), F32),
        in_specs=[vmem] * 6,
        out_specs=vmem,
        scratch_shapes=[
            pltpu.VMEM((cols, rows), BF16),
            pltpu.VMEM((nblk, 2, half, rows), BF16),
            pltpu.VMEM((2, 3, half, bnd), BF16),
            pltpu.VMEM((2, 2, 3, half, bnd), BF16),
            pltpu.VMEM((steps, 9, atoms), F32),
            pltpu.VMEM((2 * rows, rows), BF16),
            pltpu.VMEM((2 * rows, rows), BF16),
            pltpu.VMEM((2, half, rows), F32),
            pltpu.VMEM((cols, rows), BF16),
            pltpu.VMEM((nblk * cols, cols), F32),
            line, line, line, line,
            dma((2,)), dma((2,)), dma((2,)), dma((2,)),
            dma((nblk - 1,)), dma((nblk - 1,)), dma((nblk - 1,)), dma((nblk - 1,)),
            dma((n,)), dma((n,)), dma((n,)), dma((n,)),
        ],
        compiler_params=pltpu.CompilerParams(
            collective_id=0, has_side_effects=True, vmem_limit_bytes=48 * 1024 * 1024
        ),
    )(panel_vectors, force_blocks, bond_vectors, neighbours,
      boundary_low.reshape(1, bnd), boundary_high.reshape(1, bnd))
    scale = (3.0 * atoms * n) ** (-0.5)
    return (result * scale)[None, :, :]


def solution(mesh):
    in_specs = (
        P("dom", ("panel", "blk")),
        P(None, None, "dom"),
        P("dir", None, "dom"),
        P(None, "dom"),
        P("dom"),
        P("dom"),
    )
    out_specs = P("dir", ("panel", "dom"), "blk")
    return jax.shard_map(
        functools.partial(per_device, mesh.shape["dom"], mesh.shape["blk"]),
        mesh=mesh, in_specs=in_specs, out_specs=out_specs, check_vma=False
    )
```

```python
import functools

import jax
import jax.numpy as jnp
from jax import lax
from jax.experimental import pallas as pl
from jax.experimental.pallas import tpu as pltpu
from jax.sharding import PartitionSpec as P

MESH = pl.DeviceIdType.MESH
BF16 = jnp.bfloat16
F32 = jnp.float32


def one_hot(hits):
    return jnp.where(hits, 1.0, 0.0).astype(BF16)


def dot(a, b):
    return jnp.dot(a, b, preferred_element_type=F32)


def kernel(n, nblk, pieces, v_ref, force_ref, bond_ref, nbr_ref, low_ref, high_ref, out_ref,
           vt, vx, hs, ht, w, wd, st_hi, st_lo, flux, part, su, ru, sd, rd,
           h_send, h_recv, hf_send, hf_recv, x_send, x_recv, xf_send, xf_recv,
           u_send, u_recv, d_send, d_recv):
    me = lax.axis_index("dom")
    blk = lax.axis_index("blk")
    core = lax.axis_index("dir")
    rows, cols = v_ref.shape
    atoms = rows // 3
    half = cols // 2
    share = half // 2
    bnd = low_ref.shape[1]
    steps = nbr_ref.shape[0]
    tile = out_ref.shape[0]
    piece = tile // pieces
    up, down = lax.rem(me + 1, n), lax.rem(me + n - 1, n)
    peers = [{"dom": up}, {"dom": down}, {"dir": 1 - core}]
    peers += [{"blk": lax.rem(blk + o, nblk)} for o in range(1, nblk)]

    barrier = pltpu.get_barrier_semaphore()
    for peer in peers:
        pl.semaphore_signal(barrier, inc=1, device_id=peer, device_id_type=MESH)

    vt[...] = v_ref[...].T
    mine = jnp.concatenate(
        [vt[pl.ds(pl.multiple_of(h * half + core * share, share), share), :] for h in range(2)], axis=0)
    atom_row = lax.broadcasted_iota(jnp.int32, (rows, bnd), 0)
    for side, list_ref in ((0, high_ref), (1, low_ref)):
        for b in range(3):
            pick = one_hot(atom_row == 3 * list_ref[...] + b)
            rows_out = dot(mine, pick).astype(BF16)
            for h in range(2):
                hs[side, h, b] = rows_out[h * share:(h + 1) * share]
    pl.semaphore_wait(barrier, len(peers))

    halo = {
        (side, h): pltpu.make_async_remote_copy(
            src_ref=hs.at[side, h], dst_ref=ht.at[side, h, core],
            send_sem=h_send.at[2 * side + h], recv_sem=h_recv.at[2 * side + h],
            device_id={"dom": up if side == 0 else down}, device_id_type=MESH)
        for h in range(2) for side in range(2)
    }
    for copy in halo.values():
        copy.start()

    row_of = lax.broadcasted_iota(jnp.int32, (rows, atoms), 0)
    atom_of = lax.broadcasted_iota(jnp.int32, (rows, atoms), 1)
    for a in range(3):
        pick = one_hot(row_of == 3 * atom_of + a)
        for h in range(2):
            vx[blk, h, :, a * atoms:(a + 1) * atoms] = dot(vt[h * half:(h + 1) * half, :], pick).astype(BF16)

    tiles = [
        pltpu.make_async_remote_copy(
            src_ref=vx.at[blk, core], dst_ref=vx.at[blk, core],
            send_sem=x_send.at[o - 1], recv_sem=x_recv.at[o - 1],
            device_id={"blk": lax.rem(blk + o, nblk)}, device_id_type=MESH)
        for o in range(1, nblk)
    ]
    for copy in tiles:
        copy.start()

    for k in range(steps):
        w[k] = force_ref[k] * bond_ref[0, k:k + 1, :]
    for k in range(steps):
        total = w[k]
        name = jnp.broadcast_to(nbr_ref[k:k + 1, :], total.shape)
        for other in range(k):
            total = total + jnp.where(name == nbr_ref[other:other + 1, :], w[other], 0.0)
        wd[k] = total

    group = 16
    lanes = min(atoms, 256)

    def build(t, carry):
        j0 = pl.multiple_of(t * group, group)
        region = t // (atoms // group)
        base = pl.multiple_of(region * rows + (j0 - region * atoms), group)
        for i0 in range(0, atoms, lanes):
            js = lax.broadcasted_iota(jnp.int32, (group, lanes), 0) + j0
            total = [jnp.zeros((group, lanes), F32) for _ in range(9)]
            for k in range(steps):
                hit = js == nbr_ref[k:k + 1, i0:i0 + lanes]
                for q in range(9):
                    total[q] = jnp.where(hit, wd[k, q:q + 1, i0:i0 + lanes], total[q])
            for a in range(3):
                for b in range(3):
                    value = total[3 * a + b]
                    high = value.astype(BF16)
                    at = (pl.ds(pl.multiple_of(base + b * atoms, group), group),
                          slice(a * atoms + i0, a * atoms + i0 + lanes))
                    st_hi[at] = high
                    st_lo[at] = (value - high.astype(F32)).astype(BF16)
        return carry

    lax.fori_loop(0, (atoms + 2 * bnd) // group, build, 0)

    onward = {}
    tiles_on = []

    def pass_halo(h):
        for side in range(2):
            halo[side, h].wait_recv()
            onward[side, h] = pltpu.make_async_remote_copy(
                src_ref=ht.at[side, h, core], dst_ref=ht.at[side, h, core],
                send_sem=hf_send.at[2 * side + h], recv_sem=hf_recv.at[2 * side + h],
                device_id={"dir": 1 - core}, device_id_type=MESH)
            onward[side, h].start()

    def pass_tiles():
        for o in range(1, nblk):
            tiles[o - 1].wait_recv()
            source = lax.rem(blk + nblk - o, nblk)
            copy = pltpu.make_async_remote_copy(
                src_ref=vx.at[source, core], dst_ref=vx.at[source, core],
                send_sem=xf_send.at[o - 1], recv_sem=xf_recv.at[o - 1],
                device_id={"dir": 1 - core}, device_id_type=MESH)
            copy.start()
            tiles_on.append(copy)

    def term(h, e, r):
        return part[h, pl.ds(pl.multiple_of(e * tile + r * piece, piece), piece), :]

    def hop(h, e, r, out, into, send, recv, target):
        cell = (h * n + e) * pieces + r
        here = pl.ds(r * piece, piece)
        return pltpu.make_async_remote_copy(
            src_ref=out.at[h, e, here], dst_ref=into.at[h, e, here],
            send_sem=send.at[cell], recv_sem=recv.at[cell],
            device_id={"dom": target}, device_id_type=MESH)

    def rising(h, e, r):
        return hop(h, e, r, su, ru, u_send, u_recv, up)

    def falling(h, e, r):
        return hop(h, e, r, sd, rd, d_send, d_recv, down)

    def ends(t):
        return ((me, n - 1 - (t - me), rising, su, ru),
                (n - 1 - me, t - (n - 1 - me), falling, sd, rd))

    def own_flux(h):
        own = vx[blk, h]
        flux[h] = dot(own, st_hi[:rows, :]) + dot(own, st_lo[:rows, :])

    def couple(h):
        for side in range(2):
            onward[side, h].wait_recv()
        outer = jnp.concatenate(
            [jnp.concatenate([ht[side, h, c, b] for b in range(3) for side in range(2)], axis=1)
             for c in range(2)], axis=0)
        total = flux[h] + dot(outer, st_hi[rows:, :]) + dot(outer, st_lo[rows:, :])
        return total.astype(BF16)

    def multiply(h, columns):
        part[h] = lax.dot_general(
            vx[...].reshape(nblk * cols, rows), columns, (((1,), (1,)), ((), ())),
            preferred_element_type=F32)

    def emit(h):
        for t in range(n - 1):
            for first, e, make, out, into in ends(t):
                @pl.when(first == 0)
                def _(t=t, e=e, make=make, out=out):
                    for r in range(pieces):
                        out[h, e, r * piece:(r + 1) * piece] = term(h, e, r).astype(out.dtype)
                        make(h, e, r).start()

    own_flux(0)
    pass_halo(0)
    pass_tiles()
    own_flux(1)
    columns = couple(0)
    for copy in tiles_on:
        copy.wait_recv()
    multiply(0, columns)
    emit(0)
    pass_halo(1)
    multiply(1, couple(1))
    emit(1)

    for h in range(2):
        for t in range(1, n - 1):
            for r in range(pieces):
                for first, e, make, out, into in ends(t):
                    @pl.when((first > 0) & (first <= t))
                    def _(r=r, e=e, make=make, out=out, into=into):
                        here = slice(r * piece, (r + 1) * piece)
                        make(h, e, r).wait_recv()
                        out[h, e, here] = (term(h, e, r) + into[h, e, here].astype(F32)).astype(out.dtype)
                        make(h, e, r).start()

    for h in range(2):
        for r in range(pieces):
            here = slice(r * piece, (r + 1) * piece)
            there = slice(h * half, (h + 1) * half)

            @pl.when(me == 0)
            def _():
                falling(h, me, r).wait_recv()
                out_ref[here, there] = term(h, me, r) + rd[h, me, here].astype(F32)

            @pl.when(me == n - 1)
            def _():
                rising(h, me, r).wait_recv()
                out_ref[here, there] = term(h, me, r) + ru[h, me, here].astype(F32)

            @pl.when((me > 0) & (me < n - 1))
            def _():
                rising(h, me, r).wait_recv()
                falling(h, me, r).wait_recv()
                out_ref[here, there] = (
                    term(h, me, r) + ru[h, me, here].astype(F32) + rd[h, me, here].astype(F32))

    for h in range(2):
        for t in range(n - 1):
            for first, e, make, out, into in ends(t):
                @pl.when(first <= t)
                def _(e=e, make=make):
                    for r in range(pieces):
                        make(h, e, r).wait_send()

    for copy in [*halo.values(), *onward.values(), *tiles, *tiles_on]:
        copy.wait_send()


def per_device(n, nblk, panel_vectors, force_blocks, bond_vectors, neighbours, boundary_low, boundary_high):
    rows, cols = panel_vectors.shape
    atoms = rows // 3
    half = cols // 2
    bnd = boundary_low.shape[0]
    steps = neighbours.shape[0]
    tile = nblk * cols // n
    wire = BF16 if n <= 4 else F32
    vmem = pl.BlockSpec(memory_space=pltpu.VMEM)
    pieces = 2
    line = pltpu.VMEM((2, n, tile, half), wire)
    hops = pltpu.SemaphoreType.DMA((2 * n * pieces,))
    dma = pltpu.SemaphoreType.DMA
    result = pl.pallas_call(
        functools.partial(kernel, n, nblk, pieces),
        out_shape=jax.ShapeDtypeStruct((tile, cols), F32),
        in_specs=[vmem] * 6,
        out_specs=vmem,
        scratch_shapes=[
            pltpu.VMEM((cols, rows), BF16),
            pltpu.VMEM((nblk, 2, half, rows), BF16),
            pltpu.VMEM((2, 2, 3, half // 2, bnd), BF16),
            pltpu.VMEM((2, 2, 2, 3, half // 2, bnd), BF16),
            pltpu.VMEM((steps, 9, atoms), F32),
            pltpu.VMEM((steps, 9, atoms), F32),
            pltpu.VMEM((2 * rows, rows), BF16),
            pltpu.VMEM((2 * rows, rows), BF16),
            pltpu.VMEM((2, half, rows), F32),
            pltpu.VMEM((2, nblk * cols, half), F32),
            line, line, line, line,
            dma((4,)), dma((4,)), dma((4,)), dma((4,)),
            dma((nblk - 1,)), dma((nblk - 1,)), dma((nblk - 1,)), dma((nblk - 1,)),
            hops, hops, hops, hops,
        ],
        compiler_params=pltpu.CompilerParams(
            collective_id=0, has_side_effects=True, vmem_limit_bytes=48 * 1024 * 1024
        ),
    )(panel_vectors, force_blocks, bond_vectors, neighbours,
      boundary_low.reshape(1, bnd), boundary_high.reshape(1, bnd))
    scale = (3.0 * atoms * n) ** (-0.5)
    return (result * scale)[None, :, :]


def solution(mesh):
    in_specs = (
        P("dom", ("panel", "blk")),
        P(None, None, "dom"),
        P("dir", None, "dom"),
        P(None, "dom"),
        P("dom"),
        P("dom"),
    )
    out_specs = P("dir", ("panel", "dom"), "blk")
    return jax.shard_map(
        functools.partial(per_device, mesh.shape["dom"], mesh.shape["blk"]),
        mesh=mesh, in_specs=in_specs, out_specs=out_specs, check_vma=False
    )
```

```python
import functools

import jax
import jax.numpy as jnp
from jax import lax
from jax.experimental import pallas as pl
from jax.experimental.pallas import tpu as pltpu
from jax.sharding import PartitionSpec as P

MESH = pl.DeviceIdType.MESH
BF16 = jnp.bfloat16
F32 = jnp.float32


def one_hot(hits):
    return jnp.where(hits, 1.0, 0.0).astype(BF16)


def dot(a, b):
    return jnp.dot(a, b, preferred_element_type=F32)


def kernel(n, nblk, pieces, v_ref, force_ref, bond_ref, nbr_ref, low_ref, high_ref, out_ref,
           vbuf, vx, vp, pt, hs, ht, w, wd, st_hi, st_lo, flux, part, su, ru, sd, rd,
           v_sem, h_send, h_recv, hf_send, hf_recv, x_send, x_recv, xf_send, xf_recv,
           u_send, u_recv, d_send, d_recv):
    me = lax.axis_index("dom")
    blk = lax.axis_index("blk")
    core = lax.axis_index("dir")
    rows, cols = v_ref.shape
    atoms = rows // 3
    half = cols // 2
    share = half // 2
    bnd = low_ref.shape[1]
    steps = nbr_ref.shape[0]
    tile = out_ref.shape[0]
    piece = tile // pieces
    up, down = lax.rem(me + 1, n), lax.rem(me + n - 1, n)
    peers = [{"dom": up}, {"dom": down}, {"dir": 1 - core}]
    peers += [{"blk": lax.rem(blk + o, nblk)} for o in range(1, nblk)]

    fetch = pltpu.make_async_copy(v_ref, vbuf, v_sem)
    fetch.start()
    barrier = pltpu.get_barrier_semaphore()
    for peer in peers:
        pl.semaphore_signal(barrier, inc=1, device_id=peer, device_id_type=MESH)

    fetch.wait()
    turned = vbuf[...].T
    for h in range(2):
        vx[blk, h] = turned[h * half:(h + 1) * half]
    pl.semaphore_wait(barrier, len(peers))

    tiles = [
        pltpu.make_async_remote_copy(
            src_ref=vx.at[blk, core], dst_ref=vx.at[blk, core],
            send_sem=x_send.at[o - 1], recv_sem=x_recv.at[o - 1],
            device_id={"blk": lax.rem(blk + o, nblk)}, device_id_type=MESH)
        for o in range(1, nblk)
    ]
    for copy in tiles:
        copy.start()

    mine = jnp.concatenate(
        [vx[blk, h, pl.ds(pl.multiple_of(core * share, share), share), :] for h in range(2)], axis=0)
    atom_row = lax.broadcasted_iota(jnp.int32, (rows, bnd), 0)
    for side, list_ref in ((0, high_ref), (1, low_ref)):
        for b in range(3):
            pick = one_hot(atom_row == 3 * list_ref[...] + b)
            rows_out = dot(mine, pick).astype(BF16)
            for h in range(2):
                hs[side, h, b] = rows_out[h * share:(h + 1) * share]

    halo = {
        (side, h): pltpu.make_async_remote_copy(
            src_ref=hs.at[side, h], dst_ref=ht.at[side, h, core],
            send_sem=h_send.at[2 * side + h], recv_sem=h_recv.at[2 * side + h],
            device_id={"dom": up if side == 0 else down}, device_id_type=MESH)
        for h in range(2) for side in range(2)
    }
    for copy in halo.values():
        copy.start()

    row_of = lax.broadcasted_iota(jnp.int32, (rows, atoms), 0)
    atom_of = lax.broadcasted_iota(jnp.int32, (rows, atoms), 1)
    for a in range(3):
        pick = one_hot(row_of == 3 * atom_of + a)
        for h in range(2):
            vp[h, :, a * atoms:(a + 1) * atoms] = dot(vx[blk, h], pick).astype(BF16)
    atom_of = lax.broadcasted_iota(jnp.int32, (atoms, rows), 0)
    row_of = lax.broadcasted_iota(jnp.int32, (atoms, rows), 1)
    for a in range(3):
        pt[a * atoms:(a + 1) * atoms, :] = one_hot(row_of == 3 * atom_of + a)

    for k in range(steps):
        w[k] = force_ref[k] * bond_ref[0, k:k + 1, :]
    for k in range(steps):
        total = w[k]
        name = jnp.broadcast_to(nbr_ref[k:k + 1, :], total.shape)
        for other in range(k):
            total = total + jnp.where(name == nbr_ref[other:other + 1, :], w[other], 0.0)
        wd[k] = total

    group = 16
    lanes = min(atoms, 256)

    def build(t, carry):
        j0 = pl.multiple_of(t * group, group)
        region = t // (atoms // group)
        base = pl.multiple_of(region * rows + (j0 - region * atoms), group)
        for i0 in range(0, atoms, lanes):
            js = lax.broadcasted_iota(jnp.int32, (group, lanes), 0) + j0
            total = [jnp.zeros((group, lanes), F32) for _ in range(9)]
            for k in range(steps):
                hit = js == nbr_ref[k:k + 1, i0:i0 + lanes]
                for q in range(9):
                    total[q] = jnp.where(hit, wd[k, q:q + 1, i0:i0 + lanes], total[q])
            for a in range(3):
                for b in range(3):
                    value = total[3 * a + b]
                    high = value.astype(BF16)
                    at = (pl.ds(pl.multiple_of(base + b * atoms, group), group),
                          slice(a * atoms + i0, a * atoms + i0 + lanes))
                    st_hi[at] = high
                    st_lo[at] = (value - high.astype(F32)).astype(BF16)
        return carry

    lax.fori_loop(0, (atoms + 2 * bnd) // group, build, 0)

    onward = {}
    tiles_on = []

    def pass_halo(h):
        for side in range(2):
            halo[side, h].wait_recv()
            onward[side, h] = pltpu.make_async_remote_copy(
                src_ref=ht.at[side, h, core], dst_ref=ht.at[side, h, core],
                send_sem=hf_send.at[2 * side + h], recv_sem=hf_recv.at[2 * side + h],
                device_id={"dir": 1 - core}, device_id_type=MESH)
            onward[side, h].start()

    def pass_tiles():
        for o in range(1, nblk):
            tiles[o - 1].wait_recv()
            source = lax.rem(blk + nblk - o, nblk)
            copy = pltpu.make_async_remote_copy(
                src_ref=vx.at[source, core], dst_ref=vx.at[source, core],
                send_sem=xf_send.at[o - 1], recv_sem=xf_recv.at[o - 1],
                device_id={"dir": 1 - core}, device_id_type=MESH)
            copy.start()
            tiles_on.append(copy)

    def term(h, e, r):
        return part[h, pl.ds(pl.multiple_of(e * tile + r * piece, piece), piece), :]

    def hop(h, e, r, out, into, send, recv, target):
        cell = (h * n + e) * pieces + r
        here = pl.ds(r * piece, piece)
        return pltpu.make_async_remote_copy(
            src_ref=out.at[h, e, here], dst_ref=into.at[h, e, here],
            send_sem=send.at[cell], recv_sem=recv.at[cell],
            device_id={"dom": target}, device_id_type=MESH)

    def rising(h, e, r):
        return hop(h, e, r, su, ru, u_send, u_recv, up)

    def falling(h, e, r):
        return hop(h, e, r, sd, rd, d_send, d_recv, down)

    def ends(t):
        return ((me, n - 1 - (t - me), rising, su, ru),
                (n - 1 - me, t - (n - 1 - me), falling, sd, rd))

    def own_flux(h):
        own = vp[h]
        flux[h] = dot(own, st_hi[:rows, :]) + dot(own, st_lo[:rows, :])

    def couple(h):
        for side in range(2):
            onward[side, h].wait_recv()
        outer = jnp.concatenate(
            [jnp.concatenate([ht[side, h, c, b] for b in range(3) for side in range(2)], axis=1)
             for c in range(2)], axis=0)
        total = flux[h] + dot(outer, st_hi[rows:, :]) + dot(outer, st_lo[rows:, :])
        return dot(total.astype(BF16), pt[...]).astype(BF16)

    def multiply(h, columns):
        part[h] = lax.dot_general(
            vx[...].reshape(nblk * cols, rows), columns, (((1,), (1,)), ((), ())),
            preferred_element_type=F32)

    def emit(h):
        for t in range(n - 1):
            for first, e, make, out, into in ends(t):
                @pl.when(first == 0)
                def _(t=t, e=e, make=make, out=out):
                    for r in range(pieces):
                        out[h, e, r * piece:(r + 1) * piece] = term(h, e, r).astype(out.dtype)
                        make(h, e, r).start()

    own_flux(0)
    pass_halo(0)
    pass_tiles()
    own_flux(1)
    columns = couple(0)
    for copy in tiles_on:
        copy.wait_recv()
    multiply(0, columns)
    emit(0)
    pass_halo(1)
    multiply(1, couple(1))
    emit(1)

    for h in range(2):
        for t in range(1, n - 1):
            for r in range(pieces):
                for first, e, make, out, into in ends(t):
                    @pl.when((first > 0) & (first <= t))
                    def _(r=r, e=e, make=make, out=out, into=into):
                        here = slice(r * piece, (r + 1) * piece)
                        make(h, e, r).wait_recv()
                        out[h, e, here] = (term(h, e, r) + into[h, e, here].astype(F32)).astype(out.dtype)
                        make(h, e, r).start()

    for h in range(2):
        for r in range(pieces):
            here = slice(r * piece, (r + 1) * piece)
            there = slice(h * half, (h + 1) * half)

            @pl.when(me == 0)
            def _():
                falling(h, me, r).wait_recv()
                out_ref[here, there] = term(h, me, r) + rd[h, me, here].astype(F32)

            @pl.when(me == n - 1)
            def _():
                rising(h, me, r).wait_recv()
                out_ref[here, there] = term(h, me, r) + ru[h, me, here].astype(F32)

            @pl.when((me > 0) & (me < n - 1))
            def _():
                rising(h, me, r).wait_recv()
                falling(h, me, r).wait_recv()
                out_ref[here, there] = (
                    term(h, me, r) + ru[h, me, here].astype(F32) + rd[h, me, here].astype(F32))

    for h in range(2):
        for t in range(n - 1):
            for first, e, make, out, into in ends(t):
                @pl.when(first <= t)
                def _(e=e, make=make):
                    for r in range(pieces):
                        make(h, e, r).wait_send()

    for copy in [*halo.values(), *onward.values(), *tiles, *tiles_on]:
        copy.wait_send()


def per_device(n, nblk, panel_vectors, force_blocks, bond_vectors, neighbours, boundary_low, boundary_high):
    rows, cols = panel_vectors.shape
    atoms = rows // 3
    half = cols // 2
    bnd = boundary_low.shape[0]
    steps = neighbours.shape[0]
    tile = nblk * cols // n
    wire = BF16 if n <= 4 else F32
    vmem = pl.BlockSpec(memory_space=pltpu.VMEM)
    pieces = 2
    line = pltpu.VMEM((2, n, tile, half), wire)
    hops = pltpu.SemaphoreType.DMA((2 * n * pieces,))
    dma = pltpu.SemaphoreType.DMA
    result = pl.pallas_call(
        functools.partial(kernel, n, nblk, pieces),
        out_shape=jax.ShapeDtypeStruct((tile, cols), F32),
        in_specs=[pl.BlockSpec(memory_space=pl.ANY)] + [vmem] * 5,
        out_specs=vmem,
        scratch_shapes=[
            pltpu.VMEM((rows, cols), BF16),
            pltpu.VMEM((nblk, 2, half, rows), BF16),
            pltpu.VMEM((2, half, rows), BF16),
            pltpu.VMEM((rows, rows), BF16),
            pltpu.VMEM((2, 2, 3, half // 2, bnd), BF16),
            pltpu.VMEM((2, 2, 2, 3, half // 2, bnd), BF16),
            pltpu.VMEM((steps, 9, atoms), F32),
            pltpu.VMEM((steps, 9, atoms), F32),
            pltpu.VMEM((2 * rows, rows), BF16),
            pltpu.VMEM((2 * rows, rows), BF16),
            pltpu.VMEM((2, half, rows), F32),
            pltpu.VMEM((2, nblk * cols, half), F32),
            line, line, line, line,
            dma, dma((4,)), dma((4,)), dma((4,)), dma((4,)),
            dma((nblk - 1,)), dma((nblk - 1,)), dma((nblk - 1,)), dma((nblk - 1,)),
            hops, hops, hops, hops,
        ],
        compiler_params=pltpu.CompilerParams(
            collective_id=0, has_side_effects=True, vmem_limit_bytes=48 * 1024 * 1024
        ),
    )(panel_vectors, force_blocks, bond_vectors, neighbours,
      boundary_low.reshape(1, bnd), boundary_high.reshape(1, bnd))
    scale = (3.0 * atoms * n) ** (-0.5)
    return (result * scale)[None, :, :]


def solution(mesh):
    in_specs = (
        P("dom", ("panel", "blk")),
        P(None, None, "dom"),
        P("dir", None, "dom"),
        P(None, "dom"),
        P("dom"),
        P("dom"),
    )
    out_specs = P("dir", ("panel", "dom"), "blk")
    return jax.shard_map(
        functools.partial(per_device, mesh.shape["dom"], mesh.shape["blk"]),
        mesh=mesh, in_specs=in_specs, out_specs=out_specs, check_vma=False
    )
```

```python
import functools

import jax
import jax.numpy as jnp
from jax import lax
from jax.experimental import pallas as pl
from jax.experimental.pallas import tpu as pltpu
from jax.sharding import PartitionSpec as P

MESH = pl.DeviceIdType.MESH
BF16 = jnp.bfloat16
F32 = jnp.float32


def one_hot(hits):
    return jnp.where(hits, 1.0, 0.0).astype(BF16)


def dot(a, b):
    return jnp.dot(a, b, preferred_element_type=F32)


def kernel(n, nblk, pieces, v_ref, force_ref, bond_ref, nbr_ref, low_ref, high_ref, out_ref,
           vbuf, vx, vp, pt, hs, ht, w, wd, st_hi, st_lo, flux, part, su, ru, sd, rd,
           v_sem, h_send, h_recv, hf_send, hf_recv, x_send, x_recv, xf_send, xf_recv,
           u_send, u_recv, d_send, d_recv):
    me = lax.axis_index("dom")
    blk = lax.axis_index("blk")
    core = lax.axis_index("dir")
    rows, cols = v_ref.shape
    atoms = rows // 3
    half = cols // 2
    share = half // 2
    bnd = low_ref.shape[1]
    steps = nbr_ref.shape[0]
    tile = out_ref.shape[0]
    piece = tile // pieces
    up, down = lax.rem(me + 1, n), lax.rem(me + n - 1, n)
    peers = [{"dom": up}, {"dom": down}, {"dir": 1 - core}]
    peers += [{"blk": lax.rem(blk + o, nblk)} for o in range(1, nblk)]

    fetch = pltpu.make_async_copy(v_ref, vbuf, v_sem)
    fetch.start()
    barrier = pltpu.get_barrier_semaphore()
    for peer in peers:
        pl.semaphore_signal(barrier, inc=1, device_id=peer, device_id_type=MESH)

    fetch.wait()
    turned = vbuf[...].T
    for h in range(2):
        vx[blk, h] = turned[h * half:(h + 1) * half]
    pl.semaphore_wait(barrier, len(peers))

    tiles = [
        pltpu.make_async_remote_copy(
            src_ref=vx.at[blk, core], dst_ref=vx.at[blk, core],
            send_sem=x_send.at[o - 1], recv_sem=x_recv.at[o - 1],
            device_id={"blk": lax.rem(blk + o, nblk)}, device_id_type=MESH)
        for o in range(1, nblk)
    ]
    for copy in tiles:
        copy.start()

    mine = jnp.concatenate(
        [vx[blk, h, pl.ds(pl.multiple_of(core * share, share), share), :] for h in range(2)], axis=0)
    atom_row = lax.broadcasted_iota(jnp.int32, (rows, bnd), 0)
    for side, list_ref in ((0, high_ref), (1, low_ref)):
        for b in range(3):
            pick = one_hot(atom_row == 3 * list_ref[...] + b)
            rows_out = dot(mine, pick).astype(BF16)
            for h in range(2):
                hs[side, h, b] = rows_out[h * share:(h + 1) * share]

    halo = {
        (side, h): pltpu.make_async_remote_copy(
            src_ref=hs.at[side, h], dst_ref=ht.at[side, h, core],
            send_sem=h_send.at[2 * side + h], recv_sem=h_recv.at[2 * side + h],
            device_id={"dom": up if side == 0 else down}, device_id_type=MESH)
        for h in range(2) for side in range(2)
    }
    for side in range(2):
        halo[side, 0].start()

    row_of = lax.broadcasted_iota(jnp.int32, (rows, atoms), 0)
    atom_of = lax.broadcasted_iota(jnp.int32, (rows, atoms), 1)
    for a in range(3):
        pick = one_hot(row_of == 3 * atom_of + a)
        for h in range(2):
            vp[h, :, a * atoms:(a + 1) * atoms] = dot(vx[blk, h], pick).astype(BF16)
    atom_of = lax.broadcasted_iota(jnp.int32, (atoms, rows), 0)
    row_of = lax.broadcasted_iota(jnp.int32, (atoms, rows), 1)
    for a in range(3):
        pt[a * atoms:(a + 1) * atoms, :] = one_hot(row_of == 3 * atom_of + a)

    for k in range(steps):
        w[k] = force_ref[k] * bond_ref[0, k:k + 1, :]
    for k in range(steps):
        total = w[k]
        name = jnp.broadcast_to(nbr_ref[k:k + 1, :], total.shape)
        for other in range(k):
            total = total + jnp.where(name == nbr_ref[other:other + 1, :], w[other], 0.0)
        wd[k] = total

    group = 16
    lanes = min(atoms, 256)

    def build(t, carry):
        j0 = pl.multiple_of(t * group, group)
        region = t // (atoms // group)
        base = pl.multiple_of(region * rows + (j0 - region * atoms), group)
        for i0 in range(0, atoms, lanes):
            js = lax.broadcasted_iota(jnp.int32, (group, lanes), 0) + j0
            total = [jnp.zeros((group, lanes), F32) for _ in range(9)]
            for k in range(steps):
                hit = js == nbr_ref[k:k + 1, i0:i0 + lanes]
                for q in range(9):
                    total[q] = jnp.where(hit, wd[k, q:q + 1, i0:i0 + lanes], total[q])
            for a in range(3):
                for b in range(3):
                    value = total[3 * a + b]
                    high = value.astype(BF16)
                    at = (pl.ds(pl.multiple_of(base + b * atoms, group), group),
                          slice(a * atoms + i0, a * atoms + i0 + lanes))
                    st_hi[at] = high
                    st_lo[at] = (value - high.astype(F32)).astype(BF16)
        return carry

    groups = (atoms + 2 * bnd) // group
    lax.fori_loop(0, groups // 2, build, 0)
    for side in range(2):
        halo[side, 0].wait_send()
        halo[side, 1].start()
    lax.fori_loop(groups // 2, groups, build, 0)

    onward = {}
    tiles_on = []

    def pass_halo(h):
        for side in range(2):
            halo[side, h].wait_recv()
            onward[side, h] = pltpu.make_async_remote_copy(
                src_ref=ht.at[side, h, core], dst_ref=ht.at[side, h, core],
                send_sem=hf_send.at[2 * side + h], recv_sem=hf_recv.at[2 * side + h],
                device_id={"dir": 1 - core}, device_id_type=MESH)
            onward[side, h].start()

    def pass_tiles():
        for o in range(1, nblk):
            tiles[o - 1].wait_recv()
            source = lax.rem(blk + nblk - o, nblk)
            copy = pltpu.make_async_remote_copy(
                src_ref=vx.at[source, core], dst_ref=vx.at[source, core],
                send_sem=xf_send.at[o - 1], recv_sem=xf_recv.at[o - 1],
                device_id={"dir": 1 - core}, device_id_type=MESH)
            copy.start()
            tiles_on.append(copy)

    def term(h, e, r):
        return part[h, pl.ds(pl.multiple_of(e * tile + r * piece, piece), piece), :]

    def hop(h, e, r, out, into, send, recv, target):
        cell = (h * n + e) * pieces + r
        here = pl.ds(r * piece, piece)
        return pltpu.make_async_remote_copy(
            src_ref=out.at[h, e, here], dst_ref=into.at[h, e, here],
            send_sem=send.at[cell], recv_sem=recv.at[cell],
            device_id={"dom": target}, device_id_type=MESH)

    def rising(h, e, r):
        return hop(h, e, r, su, ru, u_send, u_recv, up)

    def falling(h, e, r):
        return hop(h, e, r, sd, rd, d_send, d_recv, down)

    def ends(t):
        return ((me, n - 1 - (t - me), rising, su, ru),
                (n - 1 - me, t - (n - 1 - me), falling, sd, rd))

    def own_flux(h):
        own = vp[h]
        flux[h] = dot(own, st_hi[:rows, :]) + dot(own, st_lo[:rows, :])

    def couple(h):
        for side in range(2):
            onward[side, h].wait_recv()
        outer = jnp.concatenate(
            [jnp.concatenate([ht[side, h, c, b] for b in range(3) for side in range(2)], axis=1)
             for c in range(2)], axis=0)
        total = flux[h] + dot(outer, st_hi[rows:, :]) + dot(outer, st_lo[rows:, :])
        return dot(total.astype(BF16), pt[...]).astype(BF16)

    def multiply(h, columns):
        part[h] = lax.dot_general(
            vx[...].reshape(nblk * cols, rows), columns, (((1,), (1,)), ((), ())),
            preferred_element_type=F32)

    order = [(t, h) for t in range(n - 1) for h in range(2)]

    def emit(i):
        t, h = order[i]
        for way, (first, e, make, out, into) in enumerate(ends(t)):
            @pl.when(first == 0)
            def _(way=way, e=e, make=make, out=out):
                if i >= 2:
                    t_done, h_done = order[i - 2]
                    e_done = ends(t_done)[way][1]
                    for r in range(pieces):
                        make(h_done, e_done, r).wait_send()
                for r in range(pieces):
                    out[h, e, r * piece:(r + 1) * piece] = term(h, e, r).astype(out.dtype)
                    make(h, e, r).start()

    own_flux(0)
    pass_halo(0)
    pass_tiles()
    own_flux(1)
    columns = couple(0)
    for copy in tiles_on:
        copy.wait_recv()
    multiply(0, columns)
    emit(0)
    pass_halo(1)
    multiply(1, couple(1))
    for i in range(1, len(order)):
        emit(i)

    for t in range(1, n - 1):
        for h in range(2):
            for r in range(pieces):
                for first, e, make, out, into in ends(t):
                    @pl.when((first > 0) & (first <= t))
                    def _(r=r, e=e, make=make, out=out, into=into):
                        here = slice(r * piece, (r + 1) * piece)
                        make(h, e, r).wait_recv()
                        out[h, e, here] = (term(h, e, r) + into[h, e, here].astype(F32)).astype(out.dtype)
                        make(h, e, r).start()

    for h in range(2):
        for r in range(pieces):
            here = slice(r * piece, (r + 1) * piece)
            there = slice(h * half, (h + 1) * half)

            @pl.when(me == 0)
            def _():
                falling(h, me, r).wait_recv()
                out_ref[here, there] = term(h, me, r) + rd[h, me, here].astype(F32)

            @pl.when(me == n - 1)
            def _():
                rising(h, me, r).wait_recv()
                out_ref[here, there] = term(h, me, r) + ru[h, me, here].astype(F32)

            @pl.when((me > 0) & (me < n - 1))
            def _():
                rising(h, me, r).wait_recv()
                falling(h, me, r).wait_recv()
                out_ref[here, there] = (
                    term(h, me, r) + ru[h, me, here].astype(F32) + rd[h, me, here].astype(F32))

    for i, (t, h) in enumerate(order):
        for first, e, make, out, into in ends(t):
            early = i < len(order) - 2

            @pl.when((first <= t) & (first > 0) if early else first <= t)
            def _(e=e, make=make):
                for r in range(pieces):
                    make(h, e, r).wait_send()

    for copy in [halo[0, 1], halo[1, 1], *onward.values(), *tiles, *tiles_on]:
        copy.wait_send()


def per_device(n, nblk, panel_vectors, force_blocks, bond_vectors, neighbours, boundary_low, boundary_high):
    rows, cols = panel_vectors.shape
    atoms = rows // 3
    half = cols // 2
    bnd = boundary_low.shape[0]
    steps = neighbours.shape[0]
    tile = nblk * cols // n
    wire = BF16 if n <= 4 else F32
    vmem = pl.BlockSpec(memory_space=pltpu.VMEM)
    pieces = 2
    line = pltpu.VMEM((2, n, tile, half), wire)
    hops = pltpu.SemaphoreType.DMA((2 * n * pieces,))
    dma = pltpu.SemaphoreType.DMA
    result = pl.pallas_call(
        functools.partial(kernel, n, nblk, pieces),
        out_shape=jax.ShapeDtypeStruct((tile, cols), F32),
        in_specs=[pl.BlockSpec(memory_space=pl.ANY)] + [vmem] * 5,
        out_specs=vmem,
        scratch_shapes=[
            pltpu.VMEM((rows, cols), BF16),
            pltpu.VMEM((nblk, 2, half, rows), BF16),
            pltpu.VMEM((2, half, rows), BF16),
            pltpu.VMEM((rows, rows), BF16),
            pltpu.VMEM((2, 2, 3, half // 2, bnd), BF16),
            pltpu.VMEM((2, 2, 2, 3, half // 2, bnd), BF16),
            pltpu.VMEM((steps, 9, atoms), F32),
            pltpu.VMEM((steps, 9, atoms), F32),
            pltpu.VMEM((2 * rows, rows), BF16),
            pltpu.VMEM((2 * rows, rows), BF16),
            pltpu.VMEM((2, half, rows), F32),
            pltpu.VMEM((2, nblk * cols, half), F32),
            line, line, line, line,
            dma, dma((4,)), dma((4,)), dma((4,)), dma((4,)),
            dma((nblk - 1,)), dma((nblk - 1,)), dma((nblk - 1,)), dma((nblk - 1,)),
            hops, hops, hops, hops,
        ],
        compiler_params=pltpu.CompilerParams(
            collective_id=0, has_side_effects=True, vmem_limit_bytes=48 * 1024 * 1024
        ),
    )(panel_vectors, force_blocks, bond_vectors, neighbours,
      boundary_low.reshape(1, bnd), boundary_high.reshape(1, bnd))
    scale = (3.0 * atoms * n) ** (-0.5)
    return (result * scale)[None, :, :]


def solution(mesh):
    in_specs = (
        P("dom", ("panel", "blk")),
        P(None, None, "dom"),
        P("dir", None, "dom"),
        P(None, "dom"),
        P("dom"),
        P("dom"),
    )
    out_specs = P("dir", ("panel", "dom"), "blk")
    return jax.shard_map(
        functools.partial(per_device, mesh.shape["dom"], mesh.shape["blk"]),
        mesh=mesh, in_specs=in_specs, out_specs=out_specs, check_vma=False
    )
```

```python
import functools

import jax
import jax.numpy as jnp
from jax import lax
from jax.experimental import pallas as pl
from jax.experimental.pallas import tpu as pltpu
from jax.sharding import PartitionSpec as P

MESH = pl.DeviceIdType.MESH
BF16 = jnp.bfloat16
F32 = jnp.float32


def one_hot(hits):
    return jnp.where(hits, 1.0, 0.0).astype(BF16)


def dot(a, b):
    return jnp.dot(a, b, preferred_element_type=F32)


def kernel(n, nblk, pieces, v_ref, force_ref, bond_ref, nbr_ref, low_ref, high_ref, out_ref,
           vbuf, vx, vp, pt, hs, ht, w, wd, st_hi, st_lo, flux, part, su, ru, sd, rd,
           v_sem, h_send, h_recv, hf_send, hf_recv, x_send, x_recv, xf_send, xf_recv,
           u_send, u_recv, d_send, d_recv):
    me = lax.axis_index("dom")
    blk = lax.axis_index("blk")
    core = lax.axis_index("dir")
    rows, cols = v_ref.shape
    atoms = rows // 3
    half = cols // 2
    share = half // 2
    bnd = low_ref.shape[1]
    steps = nbr_ref.shape[0]
    tile = out_ref.shape[0]
    piece = tile // pieces
    up, down = lax.rem(me + 1, n), lax.rem(me + n - 1, n)
    peers = [{"dom": up}, {"dom": down}, {"dir": 1 - core}]
    peers += [{"blk": lax.rem(blk + o, nblk)} for o in range(1, nblk)]

    fetch = pltpu.make_async_copy(v_ref, vbuf, v_sem)
    fetch.start()
    barrier = pltpu.get_barrier_semaphore()
    for peer in peers:
        pl.semaphore_signal(barrier, inc=1, device_id=peer, device_id_type=MESH)

    fetch.wait()
    turned = vbuf[...].T
    for h in range(2):
        vx[blk, h] = turned[h * half:(h + 1) * half]
    pl.semaphore_wait(barrier, len(peers))

    tiles = [
        pltpu.make_async_remote_copy(
            src_ref=vx.at[blk, core], dst_ref=vx.at[blk, core],
            send_sem=x_send.at[o - 1], recv_sem=x_recv.at[o - 1],
            device_id={"blk": lax.rem(blk + o, nblk)}, device_id_type=MESH)
        for o in range(1, nblk)
    ]
    for copy in tiles:
        copy.start()

    mine = jnp.concatenate(
        [vx[blk, h, pl.ds(pl.multiple_of(core * share, share), share), :] for h in range(2)], axis=0)
    atom_row = lax.broadcasted_iota(jnp.int32, (rows, bnd), 0)
    for side, list_ref in ((0, high_ref), (1, low_ref)):
        for b in range(3):
            pick = one_hot(atom_row == 3 * list_ref[...] + b)
            rows_out = dot(mine, pick).astype(BF16)
            for h in range(2):
                hs[side, h, b] = rows_out[h * share:(h + 1) * share]

    halo = {
        (side, h): pltpu.make_async_remote_copy(
            src_ref=hs.at[side, h], dst_ref=ht.at[side, h, core],
            send_sem=h_send.at[2 * side + h], recv_sem=h_recv.at[2 * side + h],
            device_id={"dom": up if side == 0 else down}, device_id_type=MESH)
        for h in range(2) for side in range(2)
    }
    for side in range(2):
        halo[side, 0].start()

    row_of = lax.broadcasted_iota(jnp.int32, (rows, atoms), 0)
    atom_of = lax.broadcasted_iota(jnp.int32, (rows, atoms), 1)
    for a in range(3):
        pick = one_hot(row_of == 3 * atom_of + a)
        for h in range(2):
            vp[h, :, a * atoms:(a + 1) * atoms] = dot(vx[blk, h], pick).astype(BF16)
    atom_of = lax.broadcasted_iota(jnp.int32, (atoms, rows), 0)
    row_of = lax.broadcasted_iota(jnp.int32, (atoms, rows), 1)
    for a in range(3):
        pt[a * atoms:(a + 1) * atoms, :] = one_hot(row_of == 3 * atom_of + a)

    for k in range(steps):
        w[k] = force_ref[k] * bond_ref[0, k:k + 1, :]
    for k in range(steps):
        total = w[k]
        name = jnp.broadcast_to(nbr_ref[k:k + 1, :], total.shape)
        for other in range(k):
            total = total + jnp.where(name == nbr_ref[other:other + 1, :], w[other], 0.0)
        wd[k] = total

    group = 16
    lanes = min(atoms, 256)

    def build(t, carry):
        j0 = pl.multiple_of(t * group, group)
        region = t // (atoms // group)
        base = pl.multiple_of(region * rows + (j0 - region * atoms), group)
        for i0 in range(0, atoms, lanes):
            js = lax.broadcasted_iota(jnp.int32, (group, lanes), 0) + j0
            total = [jnp.zeros((group, lanes), F32) for _ in range(9)]
            for k in range(steps):
                hit = js == nbr_ref[k:k + 1, i0:i0 + lanes]
                for q in range(9):
                    total[q] = jnp.where(hit, wd[k, q:q + 1, i0:i0 + lanes], total[q])
            for a in range(3):
                for b in range(3):
                    value = total[3 * a + b]
                    high = value.astype(BF16)
                    at = (pl.ds(pl.multiple_of(base + b * atoms, group), group),
                          slice(a * atoms + i0, a * atoms + i0 + lanes))
                    st_hi[at] = high
                    st_lo[at] = (value - high.astype(F32)).astype(BF16)
        return carry

    groups = (atoms + 2 * bnd) // group
    lax.fori_loop(0, groups // 2, build, 0)
    for side in range(2):
        halo[side, 0].wait_send()
        halo[side, 1].start()
    lax.fori_loop(groups // 2, groups, build, 0)

    onward = {}
    tiles_on = []

    def pass_halo(h):
        for side in range(2):
            halo[side, h].wait_recv()
            onward[side, h] = pltpu.make_async_remote_copy(
                src_ref=ht.at[side, h, core], dst_ref=ht.at[side, h, core],
                send_sem=hf_send.at[2 * side + h], recv_sem=hf_recv.at[2 * side + h],
                device_id={"dir": 1 - core}, device_id_type=MESH)
            onward[side, h].start()

    def pass_tiles():
        for o in range(1, nblk):
            tiles[o - 1].wait_recv()
            source = lax.rem(blk + nblk - o, nblk)
            copy = pltpu.make_async_remote_copy(
                src_ref=vx.at[source, core], dst_ref=vx.at[source, core],
                send_sem=xf_send.at[o - 1], recv_sem=xf_recv.at[o - 1],
                device_id={"dir": 1 - core}, device_id_type=MESH)
            copy.start()
            tiles_on.append(copy)

    def term(h, e, r):
        return part[h, pl.ds(pl.multiple_of(e * tile + r * piece, piece), piece), :]

    def hop(h, e, r, out, into, send, recv, target):
        cell = (h * n + e) * pieces + r
        here = pl.ds(r * piece, piece)
        return pltpu.make_async_remote_copy(
            src_ref=out.at[h, e, here], dst_ref=into.at[h, e, here],
            send_sem=send.at[cell], recv_sem=recv.at[cell],
            device_id={"dom": target}, device_id_type=MESH)

    def rising(h, e, r):
        return hop(h, e, r, su, ru, u_send, u_recv, up)

    def falling(h, e, r):
        return hop(h, e, r, sd, rd, d_send, d_recv, down)

    def ends(t):
        return ((me, n - 1 - (t - me), rising, su, ru),
                (n - 1 - me, t - (n - 1 - me), falling, sd, rd))

    def own_flux(h):
        own = vp[h]
        flux[h] = dot(own, st_hi[:rows, :]) + dot(own, st_lo[:rows, :])

    def couple(h):
        for side in range(2):
            onward[side, h].wait_recv()
        outer = jnp.concatenate(
            [jnp.concatenate([ht[side, h, c, b] for b in range(3) for side in range(2)], axis=1)
             for c in range(2)], axis=0)
        total = flux[h] + dot(outer, st_hi[rows:, :]) + dot(outer, st_lo[rows:, :])
        return dot(total.astype(BF16), pt[...]).astype(BF16)

    def multiply(h, columns):
        part[h] = lax.dot_general(
            vx[...].reshape(nblk * cols, rows), columns, (((1,), (1,)), ((), ())),
            preferred_element_type=F32)

    order = [(t, h) for t in range(n - 1) for h in range(2)]

    def emit(i):
        t, h = order[i]
        for way, (first, e, make, out, into) in enumerate(ends(t)):
            @pl.when(first == 0)
            def _(way=way, e=e, make=make, out=out):
                if i >= 2:
                    t_done, h_done = order[i - 2]
                    e_done = ends(t_done)[way][1]
                    for r in range(pieces):
                        make(h_done, e_done, r).wait_send()
                for r in range(pieces):
                    out[h, e, r * piece:(r + 1) * piece] = term(h, e, r).astype(out.dtype)
                    make(h, e, r).start()

    own_flux(0)
    pass_halo(0)
    pass_tiles()
    columns = couple(0)
    for copy in tiles_on:
        copy.wait_recv()
    multiply(0, columns)
    emit(0)
    pass_halo(1)
    own_flux(1)
    multiply(1, couple(1))
    for i in range(1, len(order)):
        emit(i)

    for t in range(1, n - 1):
        for h in range(2):
            for r in range(pieces):
                for first, e, make, out, into in ends(t):
                    @pl.when((first > 0) & (first <= t))
                    def _(r=r, e=e, make=make, out=out, into=into):
                        here = slice(r * piece, (r + 1) * piece)
                        make(h, e, r).wait_recv()
                        out[h, e, here] = (term(h, e, r) + into[h, e, here].astype(F32)).astype(out.dtype)
                        make(h, e, r).start()

    for h in range(2):
        for r in range(pieces):
            here = slice(r * piece, (r + 1) * piece)
            there = slice(h * half, (h + 1) * half)

            @pl.when(me == 0)
            def _():
                falling(h, me, r).wait_recv()
                out_ref[here, there] = term(h, me, r) + rd[h, me, here].astype(F32)

            @pl.when(me == n - 1)
            def _():
                rising(h, me, r).wait_recv()
                out_ref[here, there] = term(h, me, r) + ru[h, me, here].astype(F32)

            @pl.when((me > 0) & (me < n - 1))
            def _():
                rising(h, me, r).wait_recv()
                falling(h, me, r).wait_recv()
                out_ref[here, there] = (
                    term(h, me, r) + ru[h, me, here].astype(F32) + rd[h, me, here].astype(F32))

    for i, (t, h) in enumerate(order):
        for first, e, make, out, into in ends(t):
            early = i < len(order) - 2

            @pl.when((first <= t) & (first > 0) if early else first <= t)
            def _(e=e, make=make):
                for r in range(pieces):
                    make(h, e, r).wait_send()

    for copy in [halo[0, 1], halo[1, 1], *onward.values(), *tiles, *tiles_on]:
        copy.wait_send()


def per_device(n, nblk, panel_vectors, force_blocks, bond_vectors, neighbours, boundary_low, boundary_high):
    rows, cols = panel_vectors.shape
    atoms = rows // 3
    half = cols // 2
    bnd = boundary_low.shape[0]
    steps = neighbours.shape[0]
    tile = nblk * cols // n
    wire = BF16 if n <= 4 else F32
    vmem = pl.BlockSpec(memory_space=pltpu.VMEM)
    pieces = 2
    line = pltpu.VMEM((2, n, tile, half), wire)
    hops = pltpu.SemaphoreType.DMA((2 * n * pieces,))
    dma = pltpu.SemaphoreType.DMA
    result = pl.pallas_call(
        functools.partial(kernel, n, nblk, pieces),
        out_shape=jax.ShapeDtypeStruct((tile, cols), F32),
        in_specs=[pl.BlockSpec(memory_space=pl.ANY)] + [vmem] * 5,
        out_specs=vmem,
        scratch_shapes=[
            pltpu.VMEM((rows, cols), BF16),
            pltpu.VMEM((nblk, 2, half, rows), BF16),
            pltpu.VMEM((2, half, rows), BF16),
            pltpu.VMEM((rows, rows), BF16),
            pltpu.VMEM((2, 2, 3, half // 2, bnd), BF16),
            pltpu.VMEM((2, 2, 2, 3, half // 2, bnd), BF16),
            pltpu.VMEM((steps, 9, atoms), F32),
            pltpu.VMEM((steps, 9, atoms), F32),
            pltpu.VMEM((2 * rows, rows), BF16),
            pltpu.VMEM((2 * rows, rows), BF16),
            pltpu.VMEM((2, half, rows), F32),
            pltpu.VMEM((2, nblk * cols, half), F32),
            line, line, line, line,
            dma, dma((4,)), dma((4,)), dma((4,)), dma((4,)),
            dma((nblk - 1,)), dma((nblk - 1,)), dma((nblk - 1,)), dma((nblk - 1,)),
            hops, hops, hops, hops,
        ],
        compiler_params=pltpu.CompilerParams(
            collective_id=0, has_side_effects=True, vmem_limit_bytes=48 * 1024 * 1024
        ),
    )(panel_vectors, force_blocks, bond_vectors, neighbours,
      boundary_low.reshape(1, bnd), boundary_high.reshape(1, bnd))
    scale = (3.0 * atoms * n) ** (-0.5)
    return (result * scale)[None, :, :]


def solution(mesh):
    in_specs = (
        P("dom", ("panel", "blk")),
        P(None, None, "dom"),
        P("dir", None, "dom"),
        P(None, "dom"),
        P("dom"),
        P("dom"),
    )
    out_specs = P("dir", ("panel", "dom"), "blk")
    return jax.shard_map(
        functools.partial(per_device, mesh.shape["dom"], mesh.shape["blk"]),
        mesh=mesh, in_specs=in_specs, out_specs=out_specs, check_vma=False
    )
```

```python
import functools

import jax
import jax.numpy as jnp
from jax import lax
from jax.experimental import pallas as pl
from jax.experimental.pallas import tpu as pltpu
from jax.sharding import PartitionSpec as P

MESH = pl.DeviceIdType.MESH
BF16 = jnp.bfloat16
F32 = jnp.float32


def one_hot(hits):
    return jnp.where(hits, 1.0, 0.0).astype(BF16)


def dot(a, b):
    return jnp.dot(a, b, preferred_element_type=F32)


def kernel(n, nblk, pieces, v_ref, force_ref, bond_ref, nbr_ref, low_ref, high_ref, out_ref,
           vbuf, vx, vp, pt, hs, ht, w, wd, st_hi, st_lo, flux, part, su, ru, sd, rd,
           v_sem, h_send, h_recv, hf_send, hf_recv, x_send, x_recv, xf_send, xf_recv,
           u_send, u_recv, d_send, d_recv):
    me = lax.axis_index("dom")
    blk = lax.axis_index("blk")
    core = lax.axis_index("dir")
    rows, cols = v_ref.shape
    atoms = rows // 3
    half = cols // 2
    share = half // 2
    bnd = low_ref.shape[1]
    steps = nbr_ref.shape[0]
    tile = out_ref.shape[0]
    piece = tile // pieces
    up, down = lax.rem(me + 1, n), lax.rem(me + n - 1, n)
    peers = [{"dom": up}, {"dom": down}, {"dir": 1 - core}]
    peers += [{"blk": lax.rem(blk + o, nblk)} for o in range(1, nblk)]

    fetch = pltpu.make_async_copy(v_ref, vbuf, v_sem)
    fetch.start()
    barrier = pltpu.get_barrier_semaphore()
    for peer in peers:
        pl.semaphore_signal(barrier, inc=1, device_id=peer, device_id_type=MESH)

    fetch.wait()
    turned = vbuf[...].T
    for h in range(2):
        vx[blk, h] = turned[h * half:(h + 1) * half]
    pl.semaphore_wait(barrier, len(peers))

    tiles = [
        pltpu.make_async_remote_copy(
            src_ref=vx.at[blk, core], dst_ref=vx.at[blk, core],
            send_sem=x_send.at[o - 1], recv_sem=x_recv.at[o - 1],
            device_id={"blk": lax.rem(blk + o, nblk)}, device_id_type=MESH)
        for o in range(1, nblk)
    ]
    for copy in tiles:
        copy.start()

    mine = jnp.concatenate(
        [vx[blk, h, pl.ds(pl.multiple_of(core * share, share), share), :] for h in range(2)], axis=0)
    atom_row = lax.broadcasted_iota(jnp.int32, (rows, bnd), 0)
    for side, list_ref in ((0, high_ref), (1, low_ref)):
        for b in range(3):
            pick = one_hot(atom_row == 3 * list_ref[...] + b)
            rows_out = dot(mine, pick).astype(BF16)
            for h in range(2):
                hs[side, h, b] = rows_out[h * share:(h + 1) * share]

    halo = {
        (side, h): pltpu.make_async_remote_copy(
            src_ref=hs.at[side, h], dst_ref=ht.at[side, h, core],
            send_sem=h_send.at[2 * side + h], recv_sem=h_recv.at[2 * side + h],
            device_id={"dom": up if side == 0 else down}, device_id_type=MESH)
        for h in range(2) for side in range(2)
    }
    for side in range(2):
        halo[side, 0].start()

    row_of = lax.broadcasted_iota(jnp.int32, (rows, atoms), 0)
    atom_of = lax.broadcasted_iota(jnp.int32, (rows, atoms), 1)
    for a in range(3):
        pick = one_hot(row_of == 3 * atom_of + a)
        for h in range(2):
            vp[h, :, a * atoms:(a + 1) * atoms] = dot(vx[blk, h], pick).astype(BF16)
    atom_of = lax.broadcasted_iota(jnp.int32, (atoms, rows), 0)
    row_of = lax.broadcasted_iota(jnp.int32, (atoms, rows), 1)
    for a in range(3):
        pt[a * atoms:(a + 1) * atoms, :] = one_hot(row_of == 3 * atom_of + a)

    for k in range(steps):
        w[k] = force_ref[k] * bond_ref[0, k:k + 1, :]
    for k in range(steps):
        total = w[k]
        name = jnp.broadcast_to(nbr_ref[k:k + 1, :], total.shape)
        for other in range(k):
            total = total + jnp.where(name == nbr_ref[other:other + 1, :], w[other], 0.0)
        wd[k] = total

    group = 16
    lanes = min(atoms, 256)

    def build(t, carry):
        j0 = pl.multiple_of(t * group, group)
        region = t // (atoms // group)
        base = pl.multiple_of(region * rows + (j0 - region * atoms), group)
        for i0 in range(0, atoms, lanes):
            js = lax.broadcasted_iota(jnp.int32, (group, lanes), 0) + j0
            total = [jnp.zeros((group, lanes), F32) for _ in range(9)]
            for k in range(steps):
                hit = js == nbr_ref[k:k + 1, i0:i0 + lanes]
                for q in range(9):
                    total[q] = jnp.where(hit, wd[k, q:q + 1, i0:i0 + lanes], total[q])
            for a in range(3):
                for b in range(3):
                    value = total[3 * a + b]
                    high = value.astype(BF16)
                    at = (pl.ds(pl.multiple_of(base + b * atoms, group), group),
                          slice(a * atoms + i0, a * atoms + i0 + lanes))
                    st_hi[at] = high
                    st_lo[at] = (value - high.astype(F32)).astype(BF16)
        return carry

    groups = (atoms + 2 * bnd) // group
    lax.fori_loop(0, groups // 2, build, 0)
    for side in range(2):
        halo[side, 0].wait_send()
        halo[side, 1].start()
    lax.fori_loop(groups // 2, groups, build, 0)

    onward = {}
    tiles_on = []

    def pass_halo(h):
        for side in range(2):
            halo[side, h].wait_recv()
            onward[side, h] = pltpu.make_async_remote_copy(
                src_ref=ht.at[side, h, core], dst_ref=ht.at[side, h, core],
                send_sem=hf_send.at[2 * side + h], recv_sem=hf_recv.at[2 * side + h],
                device_id={"dir": 1 - core}, device_id_type=MESH)
            onward[side, h].start()

    def pass_tiles():
        for o in range(1, nblk):
            tiles[o - 1].wait_recv()
            source = lax.rem(blk + nblk - o, nblk)
            copy = pltpu.make_async_remote_copy(
                src_ref=vx.at[source, core], dst_ref=vx.at[source, core],
                send_sem=xf_send.at[o - 1], recv_sem=xf_recv.at[o - 1],
                device_id={"dir": 1 - core}, device_id_type=MESH)
            copy.start()
            tiles_on.append(copy)

    def term(h, e, r):
        return part[h, pl.ds(pl.multiple_of(e * tile + r * piece, piece), piece), :]

    def hop(h, e, r, out, into, send, recv, target):
        cell = (h * n + e) * pieces + r
        here = pl.ds(r * piece, piece)
        return pltpu.make_async_remote_copy(
            src_ref=out.at[h, e, here], dst_ref=into.at[h, e, here],
            send_sem=send.at[cell], recv_sem=recv.at[cell],
            device_id={"dom": target}, device_id_type=MESH)

    def rising(h, e, r):
        return hop(h, e, r, su, ru, u_send, u_recv, up)

    def falling(h, e, r):
        return hop(h, e, r, sd, rd, d_send, d_recv, down)

    def ends(t):
        return ((me, n - 1 - (t - me), rising, su, ru),
                (n - 1 - me, t - (n - 1 - me), falling, sd, rd))

    def own_flux(h):
        own = vp[h]
        flux[h] = dot(own, st_hi[:rows, :]) + dot(own, st_lo[:rows, :])

    def couple(h):
        for side in range(2):
            onward[side, h].wait_recv()
        outer = jnp.concatenate(
            [jnp.concatenate([ht[side, h, c, b] for b in range(3) for side in range(2)], axis=1)
             for c in range(2)], axis=0)
        total = flux[h] + dot(outer, st_hi[rows:, :]) + dot(outer, st_lo[rows:, :])
        return dot(total.astype(BF16), pt[...]).astype(BF16)

    def multiply(h, columns):
        part[h] = lax.dot_general(
            vx[...].reshape(nblk * cols, rows), columns, (((1,), (1,)), ((), ())),
            preferred_element_type=F32)

    order = [(t, h) for t in range(n - 1) for h in range(2)]

    def emit(i):
        t, h = order[i]
        for way, (first, e, make, out, into) in enumerate(ends(t)):
            @pl.when(first == 0)
            def _(way=way, e=e, make=make, out=out):
                if i >= 2:
                    t_done, h_done = order[i - 2]
                    e_done = ends(t_done)[way][1]
                    for r in range(pieces):
                        make(h_done, e_done, r).wait_send()
                for r in range(pieces):
                    out[h, e, r * piece:(r + 1) * piece] = term(h, e, r).astype(out.dtype)
                    make(h, e, r).start()

    own_flux(0)
    pass_halo(0)
    pass_tiles()
    own_flux(1)
    columns = couple(0)
    for copy in tiles_on:
        copy.wait_recv()
    multiply(0, columns)
    emit(0)
    pass_halo(1)
    multiply(1, couple(1))
    for i in range(1, len(order)):
        emit(i)

    for t in range(1, n - 1):
        for h in range(2):
            for r in range(pieces):
                for first, e, make, out, into in ends(t):
                    @pl.when((first > 0) & (first <= t))
                    def _(r=r, e=e, make=make, out=out, into=into):
                        here = slice(r * piece, (r + 1) * piece)
                        make(h, e, r).wait_recv()
                        out[h, e, here] = (term(h, e, r) + into[h, e, here].astype(F32)).astype(out.dtype)
                        make(h, e, r).start()

    for h in range(2):
        for r in range(pieces):
            here = slice(r * piece, (r + 1) * piece)
            there = slice(h * half, (h + 1) * half)

            @pl.when(me == 0)
            def _():
                falling(h, me, r).wait_recv()
                out_ref[here, there] = term(h, me, r) + rd[h, me, here].astype(F32)

            @pl.when(me == n - 1)
            def _():
                rising(h, me, r).wait_recv()
                out_ref[here, there] = term(h, me, r) + ru[h, me, here].astype(F32)

            @pl.when((me > 0) & (me < n - 1))
            def _():
                rising(h, me, r).wait_recv()
                falling(h, me, r).wait_recv()
                out_ref[here, there] = (
                    term(h, me, r) + ru[h, me, here].astype(F32) + rd[h, me, here].astype(F32))

    for i, (t, h) in enumerate(order):
        for first, e, make, out, into in ends(t):
            early = i < len(order) - 2

            @pl.when((first <= t) & (first > 0) if early else first <= t)
            def _(e=e, make=make):
                for r in range(pieces):
                    make(h, e, r).wait_send()

    for copy in [halo[0, 1], halo[1, 1], *onward.values(), *tiles, *tiles_on]:
        copy.wait_send()


def per_device(n, nblk, panel_vectors, force_blocks, bond_vectors, neighbours, boundary_low, boundary_high):
    rows, cols = panel_vectors.shape
    atoms = rows // 3
    half = cols // 2
    bnd = boundary_low.shape[0]
    steps = neighbours.shape[0]
    tile = nblk * cols // n
    wire = BF16 if n <= 4 else F32
    vmem = pl.BlockSpec(memory_space=pltpu.VMEM)
    pieces = 4 if tile >= 128 else 2
    line = pltpu.VMEM((2, n, tile, half), wire)
    hops = pltpu.SemaphoreType.DMA((2 * n * pieces,))
    dma = pltpu.SemaphoreType.DMA
    result = pl.pallas_call(
        functools.partial(kernel, n, nblk, pieces),
        out_shape=jax.ShapeDtypeStruct((tile, cols), F32),
        in_specs=[pl.BlockSpec(memory_space=pl.ANY)] + [vmem] * 5,
        out_specs=vmem,
        scratch_shapes=[
            pltpu.VMEM((rows, cols), BF16),
            pltpu.VMEM((nblk, 2, half, rows), BF16),
            pltpu.VMEM((2, half, rows), BF16),
            pltpu.VMEM((rows, rows), BF16),
            pltpu.VMEM((2, 2, 3, half // 2, bnd), BF16),
            pltpu.VMEM((2, 2, 2, 3, half // 2, bnd), BF16),
            pltpu.VMEM((steps, 9, atoms), F32),
            pltpu.VMEM((steps, 9, atoms), F32),
            pltpu.VMEM((2 * rows, rows), BF16),
            pltpu.VMEM((2 * rows, rows), BF16),
            pltpu.VMEM((2, half, rows), F32),
            pltpu.VMEM((2, nblk * cols, half), F32),
            line, line, line, line,
            dma, dma((4,)), dma((4,)), dma((4,)), dma((4,)),
            dma((nblk - 1,)), dma((nblk - 1,)), dma((nblk - 1,)), dma((nblk - 1,)),
            hops, hops, hops, hops,
        ],
        compiler_params=pltpu.CompilerParams(
            collective_id=0, has_side_effects=True, vmem_limit_bytes=48 * 1024 * 1024
        ),
    )(panel_vectors, force_blocks, bond_vectors, neighbours,
      boundary_low.reshape(1, bnd), boundary_high.reshape(1, bnd))
    scale = (3.0 * atoms * n) ** (-0.5)
    return (result * scale)[None, :, :]


def solution(mesh):
    in_specs = (
        P("dom", ("panel", "blk")),
        P(None, None, "dom"),
        P("dir", None, "dom"),
        P(None, "dom"),
        P("dom"),
        P("dom"),
    )
    out_specs = P("dir", ("panel", "dom"), "blk")
    return jax.shard_map(
        functools.partial(per_device, mesh.shape["dom"], mesh.shape["blk"]),
        mesh=mesh, in_specs=in_specs, out_specs=out_specs, check_vma=False
    )
```
